512 devices in a mesh: row: 16 (over z), col: 32 (over y, x, core).
Axes of the slice: x: 4, y: 4, z: 16, core: 2. Of those that a mesh axis runs over, the one named last changes fastest.
Arguments:
- tokens: bfloat16 [2048, 8192], P('row'), may hold values from -6 to 6
- gate_weight: bfloat16 [8192, 16384], P('row', 'col'), may hold values from -0.09375 to 0.09375
- up_weight: bfloat16 [8192, 16384], P('row', 'col'), may hold values from -0.09375 to 0.09375
- down_weight: bfloat16 [16384, 8192], P('col', 'row'), may hold values from -0.0625 to 0.0625
- gate_mask: int32 [64, 128], P('row', 'col'), may hold values from 0 to 1, as said below
- up_mask: int32 [64, 128], P('row', 'col'), may hold values from 0 to 1, as said below
- down_mask: int32 [128, 64], P('col', 'row'), may hold values 0 or 1
Outputs:
- mixed: bfloat16 [2048, 8192], P('col', 'row')
The draws below stay inside these ranges and needn't reach their ends.
Inputs may be any that keep to these rules, and one draw needn't show every extreme that they name: `gate_mask`: each device's block of 4 x 4 tiles keeps between 4 and 12 tiles; in each column of devices some block keeps exactly 12. `up_mask`: as for gate_mask, drawn independently.
All inputs are finite; a program needn't handle non-finite values. No bound on the sum of `down_mask` on one device may be relied on, other than what follows from the above.
Results may differ from the reference program's by a relative error of at most 0.02.
Values may be sent and summed in bfloat16 or wider, within the bound.
A program may use at most 128 MiB of HBM per device.

```python
import jax
import jax.numpy as jnp
from jax import lax

D = 8192
FF = 16384
TILE = 128
TOKENS = 2048
TILE_ROWS = 4
TILE_COLS = 4
SLOTS = 12
N_ROW = 16
N_COL = 32


def tile_pattern(key):
    count = TILE_ROWS * TILE_COLS
    lowest = count // 4
    first_key, second_key, third_key = jax.random.split(key, 3)
    kept = jax.random.randint(first_key, (N_ROW, N_COL), lowest, SLOTS + 1)
    full_row = jax.random.randint(second_key, (N_COL,), 0, N_ROW)
    kept = jnp.where(jnp.arange(N_ROW)[:, None] == full_row[None, :], SLOTS, kept)
    scores = jax.random.randint(third_key, (N_ROW, N_COL, count), 0, 1 << 20) * count + jnp.arange(count)
    ranking = jnp.argsort(jnp.argsort(scores, axis=-1), axis=-1)
    flags = (ranking < kept[:, :, None]).astype(jnp.int32)
    flags = flags.reshape(N_ROW, N_COL, TILE_ROWS, TILE_COLS).transpose(0, 2, 1, 3)
    return flags.reshape(N_ROW * TILE_ROWS, N_COL * TILE_COLS)


def draw_gate_mask(key, part):
    return tile_pattern(jax.random.fold_in(key, 11))


def draw_up_mask(key, part):
    return tile_pattern(jax.random.fold_in(key, 23))


def plant(result, own_key, low, largest):
    dims = result.shape
    place = [jax.random.randint(jax.random.fold_in(own_key, axis), (), 0, dims[axis]) for axis in range(len(dims))]
    result = result.at[tuple(place)].set(low)
    longest = dims.index(max(dims))
    place[longest] = (place[longest] + 1) % dims[longest]
    return result.at[tuple(place)].set(largest)


def shard_levels(rng, shape, shards, low, high):
    loudness = 1.0
    for dim, shards_of in shards:
        heights = jax.random.uniform(jax.random.fold_in(jax.random.fold_in(rng, 6), dim), (shards_of,), jnp.float32, low / len(shards), high / len(shards))
        loudness = loudness * jnp.repeat(jnp.exp(heights), shape[dim] // shards_of).reshape((-1,) + (1,) * (len(shape) - 1 - dim))
    return loudness


def scatter_about(key, dims, scale, reach, shards=(), kind=jnp.bfloat16):
    entries = scale * jax.random.normal(key, dims, jnp.float32)
    if shards:
        entries = entries * shard_levels(key, dims, shards, -0.22, 0.18)
    return jnp.clip(entries, -reach, reach).astype(kind)


def setup_inputs(seed: int = 0) -> dict:
    arg_keys = jax.random.split(jax.random.key(seed), 8)
    tokens = scatter_about(arg_keys[0], (TOKENS, D), 1.0, 6.0, ((0, 16),))
    gate_weight = scatter_about(arg_keys[1], (D, FF), (D // 2) ** -0.5, 0.09375, ((0, 16), (1, 32)))
    up_weight = scatter_about(arg_keys[2], (D, FF), (D // 2) ** -0.5, 0.09375, ((0, 16), (1, 32)))
    down_weight = scatter_about(arg_keys[3], (FF, D), (FF // 2) ** -0.5, 0.0625, ((0, 32), (1, 16)))
    gate_mask = draw_gate_mask(jax.random.fold_in(arg_keys[7], 71), 0)
    up_mask = draw_up_mask(jax.random.fold_in(arg_keys[7], 71), 0)
    down_mask = plant((jax.random.randint(arg_keys[6], (FF // TILE, D // TILE), 0, 2) < 1).astype(jnp.int32), jax.random.fold_in(arg_keys[6], 1), 0, 1)
    return dict(tokens=tokens, gate_weight=gate_weight, up_weight=up_weight, down_weight=down_weight, gate_mask=gate_mask, up_mask=up_mask, down_mask=down_mask)


def expand(weight, mask):
    rows, cols = weight.shape
    tile_rows, tile_cols = mask.shape
    tile = rows // tile_rows
    shaped = weight.reshape(tile_rows, tile, tile_cols, tile)
    return (shaped * mask.astype(weight.dtype)[:, None, :, None]).reshape(rows, cols)


def panel_sum(left, right, panels):
    width = left.shape[1] // panels

    def step(total, index):
        start = (index * width).astype(jnp.int32)
        part_left = lax.dynamic_slice_in_dim(left, start, width, 1)
        part_right = lax.dynamic_slice_in_dim(right, start, width, 0)
        part = jnp.dot(part_left, part_right, preferred_element_type=jnp.float32)
        part = lax.optimization_barrier(part.astype(jnp.bfloat16)).astype(jnp.float32)
        return total + part, None

    start_total = jnp.zeros((left.shape[0], right.shape[1]), jnp.float32)
    total, _ = lax.scan(step, start_total, jnp.arange(panels, dtype=jnp.int32))
    return total


def reference(tokens, gate_weight, up_weight, down_weight, gate_mask, up_mask, down_mask):
    gate = panel_sum(tokens, expand(gate_weight, gate_mask), N_ROW)
    up = panel_sum(tokens, expand(up_weight, up_mask), N_ROW)
    hidden = (jax.nn.silu(gate) * up).astype(jnp.bfloat16)
    mixed = panel_sum(hidden, expand(down_weight, down_mask), N_COL)
    return mixed.astype(jnp.bfloat16)
```

```python
import functools

import jax
import jax.numpy as jnp
from jax import lax
from jax.experimental import pallas as pl
from jax.experimental.pallas import tpu as pltpu
from jax.sharding import PartitionSpec as P


def expand(weight, mask):
    rows, cols = weight.shape
    tile_rows, tile_cols = mask.shape
    tile = rows // tile_rows
    shaped = weight.reshape(tile_rows, tile, tile_cols, tile)
    return (shaped * mask.astype(weight.dtype)[:, None, :, None]).reshape(rows, cols)


def pack_tiles(weight, mask, slots):
    rows, cols = weight.shape
    tile_rows, tile_cols = mask.shape
    tile = rows // tile_rows
    count = tile_rows * tile_cols
    tiles = (
        weight.reshape(tile_rows, tile, tile_cols, tile)
        .transpose(0, 2, 1, 3)
        .reshape(count, tile * tile)
    )
    flags = mask.reshape(count)
    place = jnp.cumsum(flags) - 1
    chosen = (place[None, :] == jnp.arange(slots, dtype=jnp.int32)[:, None]) & (flags[None, :] == 1)
    packed = jnp.dot(chosen.astype(jnp.bfloat16), tiles, preferred_element_type=jnp.float32)
    packed = packed.astype(jnp.bfloat16).reshape(slots * tile, tile)
    where_from = jnp.sum(jnp.where(chosen, jnp.arange(count, dtype=jnp.int32)[None, :], 0), axis=1)
    return packed, where_from


def sparse_kernel(pos_ref, tok_ref, w_ref, out_ref, acc_g, acc_u, tot_g, tot_u, *, slots, tile, tile_cols):
    g = pl.program_id(0)

    @pl.when(g == 0)
    def _():
        tot_g[...] = jnp.zeros_like(tot_g)
        tot_u[...] = jnp.zeros_like(tot_u)

    acc_g[...] = jnp.zeros_like(acc_g)
    acc_u[...] = jnp.zeros_like(acc_u)
    base = g * (2 * slots)
    for which, acc in ((0, acc_g), (1, acc_u)):
        for s in range(slots):
            p = pos_ref[base + which * slots + s]
            i = p // tile_cols
            j = p % tile_cols
            t = tok_ref[:, pl.ds(pl.multiple_of(i * tile, tile), tile)]
            row0 = (which * slots + s) * tile
            w = w_ref[row0:row0 + tile, :]
            cols = pl.ds(pl.multiple_of(j * tile, tile), tile)
            acc[:, cols] += jnp.dot(t, w, preferred_element_type=jnp.float32)
    tot_g[...] += acc_g[...].astype(jnp.bfloat16).astype(jnp.float32)
    tot_u[...] += acc_u[...].astype(jnp.bfloat16).astype(jnp.float32)

    @pl.when(g == pl.num_programs(0) - 1)
    def _():
        v = tot_g[...]
        out_ref[...] = (v / (1.0 + jnp.exp(-v)) * tot_u[...]).astype(out_ref.dtype)


def sparse_hidden(pos, tokens, gathered, groups, slots, tile, tile_rows, tile_cols):
    tok_rows = tokens.shape[0]
    panel = tile_rows * tile
    width = tile_cols * tile
    block_rows = gathered.shape[1]
    kernel = functools.partial(sparse_kernel, slots=slots, tile=tile, tile_cols=tile_cols)
    grid_spec = pltpu.PrefetchScalarGridSpec(
        num_scalar_prefetch=1,
        grid=(groups,),
        in_specs=[
            pl.BlockSpec((tok_rows, panel), lambda g, pos: (0, g)),
            pl.BlockSpec((None, block_rows, tile), lambda g, pos: (g, 0, 0)),
        ],
        out_specs=pl.BlockSpec((tok_rows, width), lambda g, pos: (0, 0)),
        scratch_shapes=[pltpu.VMEM((tok_rows, width), jnp.float32) for _ in range(4)],
    )
    flops = 2 * 2 * groups * slots * tok_rows * tile * tile
    return pl.pallas_call(
        kernel,
        grid_spec=grid_spec,
        out_shape=jax.ShapeDtypeStruct((tok_rows, width), jnp.bfloat16),
        compiler_params=pltpu.CompilerParams(dimension_semantics=("arbitrary",)),
        cost_estimate=pl.CostEstimate(
            flops=flops, transcendentals=tok_rows * width,
            bytes_accessed=tokens.size * 2 + gathered.size * 2 + tok_rows * width * 2),
    )(pos, tokens, gathered)


def on_device(tokens, gate_weight, up_weight, down_weight, gate_mask, up_mask, down_mask):
    tile_rows, tile_cols = gate_mask.shape
    tile = gate_weight.shape[0] // tile_rows
    slots = 3 * tile_rows * tile_cols // 4
    groups = tokens.shape[1] // gate_weight.shape[0]
    gate_packed, gate_from = pack_tiles(gate_weight, gate_mask, slots)
    up_packed, up_from = pack_tiles(up_weight, up_mask, slots)
    where = jnp.concatenate([gate_from, up_from]).astype(jnp.bfloat16)
    where_rows = jnp.zeros((8, tile), jnp.bfloat16).at[0, : 2 * slots].set(where)
    combined = jnp.concatenate([gate_packed, up_packed, where_rows], axis=0)
    gathered = lax.all_gather(combined, "row", axis=0, tiled=False)
    pos = gathered[:, 2 * slots * tile, : 2 * slots].astype(jnp.int32).reshape(-1)
    hidden = sparse_hidden(pos, tokens, gathered, groups, slots, tile, tile_rows, tile_cols)
    all_hidden = lax.all_gather(hidden, "row", axis=0, tiled=True)
    down_eff = expand(down_weight, down_mask)
    return lax.psum_scatter(
        jnp.dot(all_hidden, down_eff, preferred_element_type=jnp.float32).astype(jnp.bfloat16),
        "col",
        scatter_dimension=0,
        tiled=True,
    )


def solution(mesh):
    return jax.shard_map(
        on_device,
        mesh=mesh,
        in_specs=(
            P("row", None),
            P("row", "col"),
            P("row", "col"),
            P("col", "row"),
            P("row", "col"),
            P("row", "col"),
            P("col", "row"),
        ),
        out_specs=P("col", "row"),
        check_vma=False,
    )
```

```python
import functools

import jax
import jax.numpy as jnp
from jax import lax
from jax.experimental import pallas as pl
from jax.experimental.pallas import tpu as pltpu
from jax.sharding import PartitionSpec as P


def expand(weight, mask):
    rows, cols = weight.shape
    tile_rows, tile_cols = mask.shape
    tile = rows // tile_rows
    shaped = weight.reshape(tile_rows, tile, tile_cols, tile)
    return (shaped * mask.astype(weight.dtype)[:, None, :, None]).reshape(rows, cols)


def pack_tiles(weight, mask, slots):
    rows, cols = weight.shape
    tile_rows, tile_cols = mask.shape
    tile = rows // tile_rows
    count = tile_rows * tile_cols
    tiles = (
        weight.reshape(tile_rows, tile, tile_cols, tile)
        .transpose(0, 2, 1, 3)
        .reshape(count, tile * tile)
    )
    flags = mask.reshape(count)
    place = jnp.cumsum(flags) - 1
    chosen = (place[None, :] == jnp.arange(slots, dtype=jnp.int32)[:, None]) & (flags[None, :] == 1)
    packed = jnp.dot(chosen.astype(jnp.bfloat16), tiles, preferred_element_type=jnp.float32)
    packed = packed.astype(jnp.bfloat16).reshape(slots * tile, tile)
    where_from = jnp.sum(jnp.where(chosen, jnp.arange(count, dtype=jnp.int32)[None, :], 0), axis=1)
    return packed, where_from


def sparse_kernel(pos_ref, tok_ref, w_ref, out_ref, acc_g, acc_u, tot_g, tot_u, *, slots, tile, tile_cols):
    g = pl.program_id(0)

    @pl.when(g == 0)
    def _():
        tot_g[...] = jnp.zeros_like(tot_g)
        tot_u[...] = jnp.zeros_like(tot_u)

    acc_g[...] = jnp.zeros_like(acc_g)
    acc_u[...] = jnp.zeros_like(acc_u)
    base = g * (2 * slots)
    for which, acc in ((0, acc_g), (1, acc_u)):
        for s in range(slots):
            p = pos_ref[base + which * slots + s]
            i = p // tile_cols
            j = p % tile_cols
            t = tok_ref[:, pl.ds(pl.multiple_of(i * tile, tile), tile)]
            row0 = (which * slots + s) * tile
            w = w_ref[row0:row0 + tile, :]
            cols = pl.ds(pl.multiple_of(j * tile, tile), tile)
            acc[:, cols] += jnp.dot(t, w, preferred_element_type=jnp.float32)
    tot_g[...] += acc_g[...].astype(jnp.bfloat16).astype(jnp.float32)
    tot_u[...] += acc_u[...].astype(jnp.bfloat16).astype(jnp.float32)

    @pl.when(g == pl.num_programs(0) - 1)
    def _():
        v = tot_g[...]
        out_ref[...] = (v / (1.0 + jnp.exp(-v)) * tot_u[...]).astype(out_ref.dtype)


def sparse_hidden(pos, tokens, gathered, groups, slots, tile, tile_rows, tile_cols):
    tok_rows = tokens.shape[0]
    panel = tile_rows * tile
    width = tile_cols * tile
    block_rows = gathered.shape[1]
    kernel = functools.partial(sparse_kernel, slots=slots, tile=tile, tile_cols=tile_cols)
    grid_spec = pltpu.PrefetchScalarGridSpec(
        num_scalar_prefetch=1,
        grid=(groups,),
        in_specs=[
            pl.BlockSpec((tok_rows, panel), lambda g, pos: (0, g)),
            pl.BlockSpec((None, block_rows, tile), lambda g, pos: (g, 0, 0)),
        ],
        out_specs=pl.BlockSpec((tok_rows, width), lambda g, pos: (0, 0)),
        scratch_shapes=[pltpu.VMEM((tok_rows, width), jnp.float32) for _ in range(4)],
    )
    flops = 2 * 2 * groups * slots * tok_rows * tile * tile
    return pl.pallas_call(
        kernel,
        grid_spec=grid_spec,
        out_shape=jax.ShapeDtypeStruct((tok_rows, width), jnp.bfloat16),
        compiler_params=pltpu.CompilerParams(dimension_semantics=("arbitrary",)),
        cost_estimate=pl.CostEstimate(
            flops=flops, transcendentals=tok_rows * width,
            bytes_accessed=tokens.size * 2 + gathered.size * 2 + tok_rows * width * 2),
    )(pos, tokens, gathered)


def on_device(tokens, gate_weight, up_weight, down_weight, gate_mask, up_mask, down_mask):
    tile_rows, tile_cols = gate_mask.shape
    tile = gate_weight.shape[0] // tile_rows
    slots = 3 * tile_rows * tile_cols // 4
    groups = tokens.shape[1] // gate_weight.shape[0]
    gate_packed, gate_from = pack_tiles(gate_weight, gate_mask, slots)
    up_packed, up_from = pack_tiles(up_weight, up_mask, slots)
    where = jnp.concatenate([gate_from, up_from]).astype(jnp.bfloat16)
    where_rows = jnp.zeros((8, tile), jnp.bfloat16).at[0, : 2 * slots].set(where)
    combined = jnp.concatenate([gate_packed, up_packed, where_rows], axis=0)
    gathered = lax.all_gather(combined, "row", axis=0, tiled=False)
    pos = gathered[:, 2 * slots * tile, : 2 * slots].astype(jnp.int32).reshape(-1)
    hidden = sparse_hidden(pos, tokens, gathered, groups, slots, tile, tile_rows, tile_cols)
    all_hidden = lax.all_gather(hidden, "row", axis=0, tiled=True)
    down_eff = expand(down_weight, down_mask)
    partial = jnp.dot(all_hidden, down_eff, preferred_element_type=jnp.float32).astype(jnp.bfloat16)
    n_col = lax.axis_size("col")
    pieces = lax.all_to_all(partial, "col", 0, 0, tiled=True)
    pieces = pieces.reshape(n_col, pieces.shape[0] // n_col, pieces.shape[1])
    return jnp.sum(pieces.astype(jnp.float32), axis=0).astype(jnp.bfloat16)


def solution(mesh):
    return jax.shard_map(
        on_device,
        mesh=mesh,
        in_specs=(
            P("row", None),
            P("row", "col"),
            P("row", "col"),
            P("col", "row"),
            P("row", "col"),
            P("row", "col"),
            P("col", "row"),
        ),
        out_specs=P("col", "row"),
        check_vma=False,
    )
```
